256 devices in a mesh: seq: 64 (over z, x, core), rep: 4 (over y).
Axes of the slice: x: 4, y: 4, z: 8, core: 2. Of those that a mesh axis runs over, the one named last changes fastest.
Arguments:
- queries: bfloat16 [32768, 8192], P(('rep', 'seq')), may hold values from -6 to 6
- keys: bfloat16 [32768, 1024], P(('rep', 'seq')), may hold values from -6 to 6
- values: bfloat16 [32768, 1024], P(('rep', 'seq')), may hold values from -6 to 6
- vertical: int32 [64, 24], replicated, may hold values from -1 to 511, as said below
- slash: int32 [64, 24], replicated, may hold values from -1 to 511, as said below
Outputs:
- attention: bfloat16 [32768, 8192], P(('rep', 'seq'))
The draws below stay inside these ranges and needn't reach their ends.
Inputs may be any that keep to these rules, and one draw needn't show every extreme that they name: `vertical`: in each row the entries other than -1 come first and are distinct; every row has at least one; some row has all 24 in use. `slash`: each row begins with 0; the entries other than -1 come first and are distinct; some row has all 24 in use.
All inputs are finite; a program needn't handle non-finite values.
Results may differ from the reference program's by a relative error of at most 0.0055.
Values may be sent and summed in bfloat16 or wider, within the bound.
No kernel may reach another device: no remote copies, remote signals or barrier semaphores. Data moves between devices by JAX's collectives and lax.ppermute only.
A program may use at most 128 MiB of HBM per device.

```python
import math
import jax
import jax.numpy as jnp
from jax import lax

QUERY_HEADS = 64
KEY_VALUE_HEADS = 8
HEAD_SIZE = 128
BLOCK = 64
NV = 24
NS = 24
PROMPT_TOKENS = 32768


def mask_table(key, slot_count, leading_zero):
    block_count = PROMPT_TOKENS // BLOCK
    head_keys = jax.random.split(jax.random.fold_in(key, 3), QUERY_HEADS)

    def permuted_row(row_key):
        if leading_zero:
            return jax.random.permutation(row_key, block_count - 1)[:slot_count - 1].astype(jnp.int32) + 1
        return jax.random.permutation(row_key, block_count)[:slot_count].astype(jnp.int32)
    table = jax.vmap(permuted_row)(head_keys)
    if leading_zero:
        table = jnp.concatenate([jnp.zeros((QUERY_HEADS, 1), jnp.int32), table], axis=1)
    fixed_slot = 1 if leading_zero else 0
    heavy = jax.random.randint(jax.random.fold_in(key, 4), (), 0, QUERY_HEADS, dtype=jnp.int32)
    light = (heavy + 1) % QUERY_HEADS
    row_index = jnp.arange(QUERY_HEADS, dtype=jnp.int32)[:, None]
    slot_index = jnp.arange(slot_count, dtype=jnp.int32)[None, :]
    heavy_row = row_index == heavy
    last_block = block_count - 1
    held = table[heavy, fixed_slot]
    table = jnp.where(heavy_row & (table == last_block), held, table)
    table = jnp.where(heavy_row & (slot_index == fixed_slot), last_block, table)
    counts = jax.random.randint(jax.random.fold_in(key, 5), (QUERY_HEADS,), 1, slot_count + 1, dtype=jnp.int32)
    counts = jnp.where(row_index[:, 0] == heavy, slot_count, counts)
    counts = jnp.where(row_index[:, 0] == light, 1, counts)
    return jnp.where(slot_index < counts[:, None], table, -1).astype(jnp.int32)


def draw_vertical(key, part):
    return mask_table(jax.random.fold_in(key, 101), NV, False)


def draw_slash(key, part):
    return mask_table(jax.random.fold_in(key, 202), NS, True)


def draw_queries(key, part):
    sampled_rows = jnp.clip(jax.random.normal(jax.random.fold_in(key, 1), (PROMPT_TOKENS, QUERY_HEADS, HEAD_SIZE), jnp.float32), -6.0, 6.0)
    return sampled_rows.reshape(PROMPT_TOKENS, QUERY_HEADS * HEAD_SIZE).astype(jnp.bfloat16)


def draw_keys(key, part):
    sampled_rows = jnp.clip(jax.random.normal(jax.random.fold_in(key, 2), (PROMPT_TOKENS, KEY_VALUE_HEADS, HEAD_SIZE), jnp.float32), -6.0, 6.0)
    return sampled_rows.reshape(PROMPT_TOKENS, KEY_VALUE_HEADS * HEAD_SIZE).astype(jnp.bfloat16)


def block_levels(key, extent, pieces, smallest, high):
    loudness = 1.0
    for dim, blocks in pieces:
        heights = jax.random.uniform(jax.random.fold_in(jax.random.fold_in(key, 6), dim), (blocks,), jnp.float32, smallest / len(pieces), high / len(pieces))
        loudness = loudness * jnp.repeat(jnp.exp(heights), extent[dim] // blocks).reshape((-1,) + (1,) * (len(extent) - 1 - dim))
    return loudness


def normal_values(key, extent, deviation, reach, cuts=(), kind=jnp.bfloat16):
    drawn = deviation * jax.random.normal(key, extent, jnp.float32)
    if cuts:
        drawn = drawn * block_levels(key, extent, cuts, -0.22, 0.18)
    return jnp.clip(drawn, -reach, reach).astype(kind)


def setup_inputs(seed: int = 0) -> dict:
    seeds = jax.random.split(jax.random.key(seed), 6)
    queries = draw_queries(jax.random.fold_in(seeds[5], 71), 0)
    keys = draw_keys(jax.random.fold_in(seeds[5], 71), 0)
    values = normal_values(seeds[2], (PROMPT_TOKENS, KEY_VALUE_HEADS * HEAD_SIZE), 1.0, 6.0, ((0, 256),))
    vertical = draw_vertical(jax.random.fold_in(seeds[5], 71), 0)
    slash = draw_slash(jax.random.fold_in(seeds[5], 71), 0)
    return dict(queries=queries, keys=keys, values=values, vertical=vertical, slash=slash)


def head_attention(query_rows, key_rows, value_rows, columns, offsets):
    block_count = PROMPT_TOKENS // BLOCK
    logit_scale = 1.0 / math.sqrt(HEAD_SIZE)
    query_block_list = query_rows.reshape(block_count, BLOCK, HEAD_SIZE)
    key_blocks = key_rows.reshape(block_count, BLOCK, HEAD_SIZE)
    value_blocks = value_rows.reshape(block_count, BLOCK, HEAD_SIZE)
    blocks = jnp.arange(block_count, dtype=jnp.int32)
    within = jnp.arange(BLOCK, dtype=jnp.int32)
    causal = within[None, :] <= within[:, None]
    column_ok = (columns >= 0)[None, :] & (columns[None, :] <= blocks[:, None])
    sources = blocks[:, None] - offsets[None, :]
    repeated = jnp.any(sources[:, :, None] == columns[None, None, :], axis=2)
    offset_ok = (offsets >= 0)[None, :] & (sources >= 0) & jnp.logical_not(repeated)
    picked = jnp.concatenate([jnp.broadcast_to(columns[None, :], (block_count, columns.shape[0])), sources], axis=1).astype(jnp.int32)
    picked_ok = jnp.concatenate([column_ok, offset_ok], axis=1)
    safe_pick = jnp.clip(picked, 0, block_count - 1).astype(jnp.int32)
    group_size = math.gcd(block_count, 64)

    def one_group(group_start):
        current_rows = lax.dynamic_slice_in_dim(query_block_list, group_start, group_size, 0).astype(jnp.float32)
        picks_here = lax.dynamic_slice_in_dim(safe_pick, group_start, group_size, 0)
        raw_here = lax.dynamic_slice_in_dim(picked, group_start, group_size, 0)
        ok_here = lax.dynamic_slice_in_dim(picked_ok, group_start, group_size, 0)
        blocks_here = lax.dynamic_slice_in_dim(blocks, group_start, group_size, 0)
        key_selected = key_blocks[picks_here].astype(jnp.float32)
        value_selected = value_blocks[picks_here].astype(jnp.float32)
        attention_logits = jnp.einsum('zja,zmga->zjmg', current_rows, key_selected) * logit_scale
        earlier = (raw_here < blocks_here[:, None])[:, None, :, None]
        token_ok = ok_here[:, None, :, None] & (earlier | causal[None, :, None, :])
        masked = jnp.where(token_ok, attention_logits, -jnp.inf)
        row_top = lax.optimization_barrier(jnp.max(masked, axis=(2, 3), keepdims=True))
        softmax_weights = jnp.where(token_ok, jnp.exp(masked - row_top), 0.0)
        totals = lax.optimization_barrier(jnp.sum(softmax_weights, axis=(2, 3)))
        rounded_length = lax.optimization_barrier(softmax_weights.astype(jnp.bfloat16)).astype(jnp.float32)
        blended_values = jnp.einsum('xgmj,xmjf->xgf', rounded_length, value_selected)
        return (blended_values / totals[..., None]).astype(jnp.bfloat16)
    group_starts = jnp.arange(0, block_count, group_size, dtype=jnp.int32)
    results = lax.map(one_group, group_starts)
    return results.reshape(PROMPT_TOKENS, HEAD_SIZE)

def reference(queries, keys, values, vertical, slash):
    query_heads = queries.reshape(PROMPT_TOKENS, QUERY_HEADS, HEAD_SIZE)
    key_head_group = keys.reshape(PROMPT_TOKENS, KEY_VALUE_HEADS, HEAD_SIZE)
    value_head_group = values.reshape(PROMPT_TOKENS, KEY_VALUE_HEADS, HEAD_SIZE)
    heads_per_group = QUERY_HEADS // KEY_VALUE_HEADS

    def one_head(head_index):
        key_head = head_index // heads_per_group
        return head_attention(query_heads[:, head_index], key_head_group[:, key_head], value_head_group[:, key_head], vertical[head_index], slash[head_index])
    results = lax.map(one_head, jnp.arange(QUERY_HEADS, dtype=jnp.int32))
    return jnp.transpose(results, (1, 0, 2)).reshape(PROMPT_TOKENS, QUERY_HEADS * HEAD_SIZE)
```

```python
import functools
import math

import jax
import jax.numpy as jnp
from jax import lax
from jax.experimental import pallas as pl
from jax.experimental.pallas import tpu as pltpu
from jax.sharding import Mesh, PartitionSpec as P

QUERY_HEADS = 64
KEY_VALUE_HEADS = 8
HEADS = QUERY_HEADS // KEY_VALUE_HEADS
HEAD_SIZE = 128
BLOCK = 64
ROWS = 128
SLOTS = 48
TILES = 8
CHUNK = 8
NEG_FILL = -1e30
SCALE = math.log2(math.e) / math.sqrt(HEAD_SIZE)


def attend_kernel(
    tiles, idx_ref, count_ref, query_ref, key_hbm, value_hbm, out_ref, keys, values, score_s, sem
):
    width = CHUNK * BLOCK
    key_copy = pltpu.make_async_copy(key_hbm, keys, sem.at[0])
    value_copy = pltpu.make_async_copy(value_hbm, values, sem.at[1])
    key_copy.start()
    value_copy.start()
    key_copy.wait()
    lane = lax.broadcasted_iota(jnp.int32, (BLOCK, width), 1)
    row = lax.broadcasted_iota(jnp.int32, (BLOCK, width), 0)
    causal = (lane >= BLOCK) | (lane <= row)
    groups = tiles // TILES

    def fold(op, x):
        return functools.reduce(op, [x[:, a : a + 128] for a in range(0, width, 128)])

    def group(step, _):
        head = step // groups
        first_tile = (step % groups) * TILES
        lanes = pl.ds(pl.multiple_of(head * HEAD_SIZE, HEAD_SIZE), HEAD_SIZE)
        rows = [pl.ds((first_tile + t) * BLOCK, BLOCK) for t in range(TILES)]
        lists = [head * tiles + first_tile + t for t in range(TILES)]
        counts = [count_ref[x] for x in lists]
        chunks = (functools.reduce(jnp.maximum, counts) + CHUNK - 1) // CHUNK
        query = [query_ref[r, lanes] for r in rows]

        def gathered(ref, t, c):
            starts = [pl.multiple_of(idx_ref[lists[t], c * CHUNK + j], BLOCK) for j in range(CHUNK)]
            return jnp.concatenate([ref[pl.ds(s, BLOCK), :] for s in starts], axis=0)

        def score(c, best, first):
            out = []
            for t in range(TILES):
                s = lax.dot_general(
                    query[t],
                    gathered(keys, t, c),
                    (((1,), (1,)), ((), ())),
                    preferred_element_type=jnp.float32,
                )
                ok = lane < (counts[t] - c * CHUNK) * BLOCK
                if first:
                    ok = ok & causal
                s = jnp.where(ok, s, NEG_FILL)
                score_s[t, c] = s
                top = fold(jnp.maximum, s)
                out.append(top if first else jnp.maximum(best[t], top))
            return tuple(out)

        best = score(0, None, True)
        best = lax.fori_loop(1, chunks, lambda c, b: score(c, b, False), best)
        shift = [jnp.max(b, axis=1, keepdims=True) * SCALE for b in best]

        @pl.when(step == 0)
        def _():
            value_copy.wait()

        def mix(c, carried, first):
            out = []
            for t in range(TILES):
                p = jnp.exp2(score_s[t, c] * SCALE - shift[t])
                total = fold(jnp.add, p)
                mixed = jnp.dot(
                    p.astype(jnp.bfloat16),
                    gathered(values, t, c),
                    preferred_element_type=jnp.float32,
                )
                out.append(
                    (total, mixed) if first else (carried[t][0] + total, carried[t][1] + mixed)
                )
            return tuple(out)

        state = mix(0, None, True)
        state = lax.fori_loop(1, chunks, lambda c, s: mix(c, s, False), state)
        for t in range(TILES):
            total, mixed = state[t]
            share = 1.0 / jnp.sum(total, axis=1, keepdims=True)
            out_ref[rows[t], lanes] = (mixed * share).astype(jnp.bfloat16)
        return 0

    lax.fori_loop(0, HEADS * groups, group, 0)


def attend(idx, count, query_rows, key_rows, value_rows):
    tiles = query_rows.shape[0] // BLOCK
    tokens = key_rows.shape[0]
    smem = pl.BlockSpec(memory_space=pltpu.SMEM)
    vmem = pl.BlockSpec(memory_space=pltpu.VMEM)
    hbm = pl.BlockSpec(memory_space=pl.ANY)
    return pl.pallas_call(
        functools.partial(attend_kernel, tiles),
        out_shape=jax.ShapeDtypeStruct(query_rows.shape, jnp.bfloat16),
        in_specs=[smem, smem, vmem, hbm, hbm],
        out_specs=vmem,
        scratch_shapes=[
            pltpu.VMEM((tokens, HEAD_SIZE), jnp.bfloat16),
            pltpu.VMEM((tokens, HEAD_SIZE), jnp.bfloat16),
            pltpu.VMEM((TILES, SLOTS // CHUNK, BLOCK, CHUNK * BLOCK), jnp.float32),
            pltpu.SemaphoreType.DMA((2,)),
        ],
        compiler_params=pltpu.CompilerParams(vmem_limit_bytes=40 << 20),
    )(idx, count, query_rows, key_rows, value_rows)


def block_lists(vertical, slash, sizes):
    planes, across, cores, _ = sizes
    z, x = lax.axis_index("z"), lax.axis_index("x")
    core, y = lax.axis_index("core"), lax.axis_index("rep")
    per = ROWS // BLOCK
    tiles = planes * per
    columns = lax.dynamic_slice_in_dim(vertical, z * HEADS, HEADS, 0)
    offsets = lax.dynamic_slice_in_dim(slash, z * HEADS, HEADS, 0)
    tile = jnp.arange(tiles, dtype=jnp.int32)
    strip = ((y * planes + tile // per) * across + x) * cores + core
    blocks = strip * per + tile % per
    sources = blocks[None, :, None] - offsets[:, None, :]
    repeated = jnp.any(sources[..., None] == columns[:, None, None, :], axis=-1)
    keep_source = (offsets >= 0)[:, None, :] & (sources >= 0)
    keep_source &= (offsets == 0)[:, None, :] | ~repeated
    spread = jnp.broadcast_to(columns[:, None, :], sources.shape)
    keep_column = (spread >= 0) & (spread < blocks[None, :, None])
    picks = jnp.concatenate([sources, spread], axis=-1).reshape(HEADS * tiles, SLOTS)
    keep = jnp.concatenate([keep_source, keep_column], axis=-1).reshape(HEADS * tiles, SLOTS)
    slot = jnp.arange(SLOTS, dtype=jnp.int32)
    place = jnp.sum((keep[:, None, :] & (slot[None, :] < slot[:, None])[None]).astype(jnp.int32), -1)
    half = picks % per
    strip = picks // per
    core_of = strip % cores
    x_of = strip // cores % across
    z_of = strip // (cores * across) % planes
    y_of = strip // (cores * across * planes)
    where = ((((y_of * across + x_of) * cores + core_of) * planes + z_of) * per + half) * BLOCK
    hit = keep[:, None, :] & (place[:, None, :] == slot[None, :, None])
    idx = jnp.sum(jnp.where(hit, where[:, None, :], 0), axis=-1)
    return idx, jnp.sum(keep.astype(jnp.int32), axis=-1)


def body(sizes, queries, keys, values, vertical, slash):
    planes = sizes[0]
    idx, count = block_lists(vertical, slash, sizes)

    def regroup(x):
        x = x.reshape(ROWS, planes, -1).transpose(1, 0, 2)
        return lax.all_to_all(x, "z", split_axis=0, concat_axis=0, tiled=True)

    def whole(x):
        x = regroup(x).reshape(planes * ROWS, HEAD_SIZE)
        return lax.all_gather(x, ("rep", "x", "core"), axis=0, tiled=True)

    key_rows, value_rows = whole(keys), whole(values)
    query_rows = regroup(queries).reshape(planes * ROWS, HEADS * HEAD_SIZE)
    out = attend(idx, count, query_rows, key_rows, value_rows)
    out = lax.all_to_all(
        out.reshape(planes, ROWS, HEADS * HEAD_SIZE), "z", split_axis=0, concat_axis=0, tiled=True
    )
    return out.transpose(1, 0, 2).reshape(ROWS, QUERY_HEADS * HEAD_SIZE)


def solution(mesh):
    reps = mesh.devices.shape[1]
    sizes = (8, 4, 2, reps)
    split = Mesh(mesh.devices.reshape(sizes), ("z", "x", "core", "rep"))
    rows = P(("rep", "z", "x", "core"), None)
    return jax.shard_map(
        functools.partial(body, sizes),
        mesh=split,
        in_specs=(rows, rows, rows, P(), P()),
        out_specs=rows,
        check_vma=False,
    )
```

```python
import functools
import math

import jax
import jax.numpy as jnp
from jax import lax
from jax.experimental import pallas as pl
from jax.experimental.pallas import tpu as pltpu
from jax.sharding import Mesh, PartitionSpec as P

QUERY_HEADS = 64
KEY_VALUE_HEADS = 8
HEADS = QUERY_HEADS // KEY_VALUE_HEADS
HEAD_SIZE = 128
BLOCK = 64
ROWS = 128
SLOTS = 48
TILES = 8
CHUNK = 8
HEAD_CUTS = (0, 4, 8)
NEG_FILL = -1e30
SCALE = math.log2(math.e) / math.sqrt(HEAD_SIZE)


def attend_kernel(
    tiles, first_head, heads, key_at, value_at, idx_ref, count_ref, query_ref, *refs
):
    pieces, refs = refs[: len(key_at) + len(value_at)], refs[len(key_at) + len(value_at) :]
    out_ref, keys, values, scores_a, scores_b, shift_a, shift_b, sem = refs
    score_s, shift_s = (scores_a, scores_b), (shift_a, shift_b)
    width = CHUNK * BLOCK
    slots = iter(range(sem.shape[0]))

    def copies(sources, places, target):
        return [
            pltpu.make_async_copy(
                source.at[pl.ds(a, n), :], target.at[pl.ds(b, n), :], sem.at[next(slots)]
            )
            for source, place in zip(sources, places)
            for a, b, n in place
        ]

    key_copies = copies(pieces[: len(key_at)], key_at, keys)
    value_copies = copies(pieces[len(key_at) :], value_at, values)
    for copy in key_copies + value_copies:
        copy.start()
    for copy in key_copies:
        copy.wait()
    lane = lax.broadcasted_iota(jnp.int32, (1, width), 1)
    wide = lax.broadcasted_iota(jnp.int32, (BLOCK, width), 1)
    causal = (wide >= BLOCK) | (wide <= lax.broadcasted_iota(jnp.int32, (BLOCK, width), 0))
    groups = tiles // TILES
    steps = heads * groups
    every = range(TILES)

    def fold(op, x):
        return functools.reduce(op, [x[:, a : a + 128] for a in range(0, width, 128)])

    def list_of(step, t):
        return (first_head + step // groups) * tiles + (step % groups) * TILES + t

    def place_of(step, t):
        head = step // groups
        return (
            pl.ds(((step % groups) * TILES + t) * BLOCK, BLOCK),
            pl.ds(pl.multiple_of(head * HEAD_SIZE, HEAD_SIZE), HEAD_SIZE),
        )

    def chunks_of(step):
        counts = [count_ref[list_of(step, t)] for t in every]
        return (functools.reduce(jnp.maximum, counts) + CHUNK - 1) // CHUNK

    def gathered(ref, at, c):
        starts = [pl.multiple_of(idx_ref[at, c * CHUNK + j], BLOCK) for j in range(CHUNK)]
        return jnp.concatenate([ref[pl.ds(s, BLOCK), :] for s in starts], axis=0)

    def score(step, side, c, t, best):
        at = list_of(step, t)
        s = lax.dot_general(
            query_ref[place_of(step, t)],
            gathered(keys, at, c),
            (((1,), (1,)), ((), ())),
            preferred_element_type=jnp.float32,
        )
        ok = lane < (count_ref[at] - c * CHUNK) * BLOCK
        if best is None:
            ok = ok & causal
        s = jnp.where(ok, s, NEG_FILL)
        score_s[side][t, c] = s
        top = fold(jnp.maximum, s)
        return top if best is None else jnp.maximum(best, top)

    def mix(step, side, c, t, state):
        shift = jnp.concatenate([shift_s[side][t]] * (width // 128), axis=1)
        p = jnp.exp2(score_s[side][t, c] * SCALE - shift)
        total = fold(jnp.add, p)
        mixed = jnp.dot(
            p.astype(jnp.bfloat16),
            gathered(values, list_of(step, t), c),
            preferred_element_type=jnp.float32,
        )
        return (total, mixed) if state is None else (state[0] + total, state[1] + mixed)

    def settle(side, best):
        for t in every:
            top = jnp.max(best[t], axis=1, keepdims=True) * SCALE
            shift_s[side][t] = jnp.broadcast_to(top, (BLOCK, 128))

    def more_scores(step, side, start, end, best):
        def more(c, best):
            return tuple(score(step, side, c, t, best[t]) for t in every)

        return lax.fori_loop(start, end, more, best)

    best = tuple(score(0, 0, 0, t, None) for t in every)
    settle(0, more_scores(0, 0, 1, chunks_of(0), best))
    for copy in value_copies:
        copy.wait()

    def one_step(step, side):
        other = 1 - side
        later = jnp.minimum(step + 1, steps - 1)
        here = chunks_of(step)
        there = jnp.where(step + 1 < steps, chunks_of(later), 1)
        both = [(mix(step, side, 0, t, None), score(later, other, 0, t, None)) for t in every]

        def fused(c, carried):
            state, best = carried
            both = [
                (mix(step, side, c, t, state[t]), score(later, other, c, t, best[t]))
                for t in every
            ]
            return tuple(x[0] for x in both), tuple(x[1] for x in both)

        shared = jnp.minimum(here, there)
        state, best = lax.fori_loop(
            1, shared, fused, (tuple(x[0] for x in both), tuple(x[1] for x in both))
        )
        state = lax.fori_loop(
            shared, here, lambda c, st: tuple(mix(step, side, c, t, st[t]) for t in every), state
        )
        best = more_scores(later, other, shared, there, best)
        for t in every:
            total, mixed = state[t]
            share = 1.0 / jnp.sum(total, axis=1, keepdims=True)
            out_ref[place_of(step, t)] = (mixed * share).astype(jnp.bfloat16)
        settle(other, best)

    def two_steps(pair, _):
        one_step(2 * pair, 0)
        one_step(2 * pair + 1, 1)
        return 0

    lax.fori_loop(0, steps // 2, two_steps, 0)


def attend(first_head, idx, count, query_rows, key_pieces, value_pieces, key_at, value_at, tokens):
    tiles = query_rows.shape[0] // BLOCK
    heads = query_rows.shape[1] // HEAD_SIZE
    smem = pl.BlockSpec(memory_space=pltpu.SMEM)
    vmem = pl.BlockSpec(memory_space=pltpu.VMEM)
    hbm = pl.BlockSpec(memory_space=pl.ANY)
    return pl.pallas_call(
        functools.partial(attend_kernel, tiles, first_head, heads, key_at, value_at),
        out_shape=jax.ShapeDtypeStruct(query_rows.shape, jnp.bfloat16),
        in_specs=[smem, smem, vmem] + [hbm] * (len(key_pieces) + len(value_pieces)),
        out_specs=vmem,
        scratch_shapes=[
            pltpu.VMEM((tokens, HEAD_SIZE), jnp.bfloat16),
            pltpu.VMEM((tokens, HEAD_SIZE), jnp.bfloat16),
            pltpu.VMEM((TILES, SLOTS // CHUNK, BLOCK, CHUNK * BLOCK), jnp.float32),
            pltpu.VMEM((TILES, SLOTS // CHUNK, BLOCK, CHUNK * BLOCK), jnp.float32),
            pltpu.VMEM((TILES, BLOCK, 128), jnp.float32),
            pltpu.VMEM((TILES, BLOCK, 128), jnp.float32),
            pltpu.SemaphoreType.DMA((sum(len(x) for x in key_at + value_at),)),
        ],
        compiler_params=pltpu.CompilerParams(vmem_limit_bytes=40 << 20),
    )(idx, count, query_rows, *key_pieces, *value_pieces)


def shifted(x, axis, size, by):
    return lax.ppermute(x, axis, [(i, (i + by) % size) for i in range(size)])


def ring_slot(distance, size):
    step = distance % size
    return jnp.where(step == 3, 1, jnp.where(step == 0, 0, step + 1))


def both_ways(xs, axes, beside=()):
    out = [shifted(x, axis, 4, by) for x, axis in zip(xs, axes) for by in (1, -1)]
    out = lax.optimization_barrier(tuple(xs) + tuple(out) + tuple(beside))
    xs, out, beside = out[:2], out[2:6], out[6:]
    return xs, out[::2], out[1::2], beside


def onward(previous, following, axes):
    out = []
    for p, f, axis in zip(previous, following, axes):
        half = p.shape[0] // 2
        out.append(shifted(p[:half], axis, 4, 1))
        out.append(shifted(f[half:], axis, 4, -1))
    return out


def block_lists(vertical, slash, sizes):
    planes, across, cores, reps = sizes
    z, x = lax.axis_index("z"), lax.axis_index("x")
    core, y = lax.axis_index("core"), lax.axis_index("rep")
    per = ROWS // BLOCK
    tiles = planes * per
    columns = lax.dynamic_slice_in_dim(vertical, z * HEADS, HEADS, 0)
    offsets = lax.dynamic_slice_in_dim(slash, z * HEADS, HEADS, 0)
    tile = jnp.arange(tiles, dtype=jnp.int32)
    strip = ((y * planes + tile // per) * across + x) * cores + core
    blocks = strip * per + tile % per
    sources = blocks[None, :, None] - offsets[:, None, :]
    repeated = jnp.any(sources[..., None] == columns[:, None, None, :], axis=-1)
    keep_source = (offsets >= 0)[:, None, :] & (sources >= 0)
    keep_source &= (offsets == 0)[:, None, :] | ~repeated
    spread = jnp.broadcast_to(columns[:, None, :], sources.shape)
    keep_column = (spread >= 0) & (spread < blocks[None, :, None])
    picks = jnp.concatenate([sources, spread], axis=-1).reshape(HEADS * tiles, SLOTS)
    keep = jnp.concatenate([keep_source, keep_column], axis=-1).reshape(HEADS * tiles, SLOTS)
    slot = jnp.arange(SLOTS, dtype=jnp.int32)
    place = jnp.sum((keep[:, None, :] & (slot[None, :] < slot[:, None])[None]).astype(jnp.int32), -1)
    half = picks % per
    strip = picks // per
    core_of = (strip + core) % cores
    x_of = ring_slot(strip // cores - x, across)
    z_of = strip // (cores * across) % planes
    y_of = ring_slot(strip // (cores * across * planes) - y, reps)
    where = ((((core_of * reps + y_of) * across + x_of) * planes + z_of) * per + half) * BLOCK
    hit = keep[:, None, :] & (place[:, None, :] == slot[None, :, None])
    idx = jnp.sum(jnp.where(hit, where[:, None, :], 0), axis=-1)
    return idx, jnp.sum(keep.astype(jnp.int32), axis=-1)


def body(sizes, queries, keys, values, vertical, slash):
    planes, across, cores, reps = sizes
    idx, count = block_lists(vertical, slash, sizes)

    def regroup(x):
        return lax.all_to_all(x, "z", split_axis=0, concat_axis=0, tiled=True)

    def by_plane(x):
        return x.reshape(ROWS, planes, -1).transpose(1, 0, 2)

    pair = regroup(jnp.concatenate([by_plane(keys), by_plane(values)], axis=1))
    own = planes * ROWS
    key_rows = pair[:, :ROWS].reshape(own, HEAD_SIZE)
    value_rows = pair[:, ROWS:].reshape(own, HEAD_SIZE)
    axes = ("x", "rep")
    xs, previous, following, _ = both_ways((key_rows, value_rows), axes)
    far = lax.optimization_barrier(tuple(onward(previous, following, axes)))
    xs = [
        jnp.concatenate([xs[i], previous[i], following[i], far[2 * i], far[2 * i + 1]], axis=0)
        for i in range(2)
    ]
    axes = ("rep", "x")
    *xs, queries = lax.optimization_barrier((*xs, queries))
    query_rows = regroup(by_plane(queries)).reshape(own, HEADS * HEAD_SIZE)
    cuts = [a * HEAD_SIZE for a in HEAD_CUTS]
    query_parts = [query_rows[:, a:b] for a, b in zip(cuts, cuts[1:])]
    beside = (idx, count, *[shifted(x, "core", cores, 1) for x in xs])
    xs, previous, following, beside = both_ways(xs, axes, beside)
    idx, count, *across_core = beside
    far = onward(previous, following, axes)
    pieces = []
    for i in range(2):
        near = [xs[i], previous[i], following[i]]
        other = [across_core[i]] + [shifted(p, "core", cores, 1) for p in near[1:]]
        pieces.append((near + far[2 * i : 2 * i + 2], other))
    far = lax.optimization_barrier(tuple(far))
    for i in range(2):
        last = [shifted(p, "core", cores, 1) for p in far[2 * i : 2 * i + 2]]
        pieces[i] = pieces[i][0] + pieces[i][1] + last
    key_pieces, value_pieces = pieces

    key_at, value_at = [], []
    place = 0
    for piece in key_pieces:
        key_at.append([(0, place, piece.shape[0])])
        place += piece.shape[0]
    place = 0
    for piece in value_pieces:
        parts = []
        for a in range(0, piece.shape[0], own):
            core_of, rest = divmod((place + a) // own, across * reps)
            x_of, y_of = divmod(rest, reps)
            parts.append((a, ((core_of * reps + y_of) * across + x_of) * own, own))
        value_at.append(parts)
        place += piece.shape[0]

    outs = []
    first_head = 0
    for query_rows in query_parts:
        out = attend(
            first_head, idx, count, query_rows, key_pieces, value_pieces, key_at, value_at, place
        )
        first_head += query_rows.shape[1] // HEAD_SIZE
        outs.append(regroup(out.reshape(planes, ROWS, query_rows.shape[1])))
    out = jnp.concatenate(outs, axis=2)
    return out.transpose(1, 0, 2).reshape(ROWS, QUERY_HEADS * HEAD_SIZE)


def solution(mesh):
    reps = mesh.devices.shape[1]
    sizes = (8, 4, 2, reps)
    split = Mesh(mesh.devices.reshape(sizes), ("z", "x", "core", "rep"))
    rows = P(("rep", "z", "x", "core"), None)
    return jax.shard_map(
        functools.partial(body, sizes),
        mesh=split,
        in_specs=(rows, rows, rows, P(), P()),
        out_specs=rows,
        check_vma=False,
    )
```

```python
import functools
import math

import jax
import jax.numpy as jnp
from jax import lax
from jax.experimental import pallas as pl
from jax.experimental.pallas import tpu as pltpu
from jax.sharding import Mesh, PartitionSpec as P

QUERY_HEADS = 64
KEY_VALUE_HEADS = 8
HEADS = QUERY_HEADS // KEY_VALUE_HEADS
HEAD_SIZE = 128
BLOCK = 64
ROWS = 128
SLOTS = 48
TILES = 8
CHUNK = 8
HEAD_CUTS = (0, 4, 8)
NEG_FILL = -1e30
SCALE = math.log2(math.e) / math.sqrt(HEAD_SIZE)


def attend_kernel(
    tiles, first_head, heads, key_at, value_at, idx_ref, count_ref, query_ref, *refs
):
    pieces, refs = refs[: len(key_at) + len(value_at)], refs[len(key_at) + len(value_at) :]
    out_ref, keys, values, scores_a, scores_b, shift_a, shift_b, sem = refs
    score_s, shift_s = (scores_a, scores_b), (shift_a, shift_b)
    width = CHUNK * BLOCK
    slots = iter(range(sem.shape[0]))

    def copies(sources, places, target):
        return [
            pltpu.make_async_copy(
                source.at[pl.ds(a, n), :], target.at[pl.ds(b, n), :], sem.at[next(slots)]
            )
            for source, place in zip(sources, places)
            for a, b, n in place
        ]

    key_copies = copies(pieces[: len(key_at)], key_at, keys)
    value_copies = copies(pieces[len(key_at) :], value_at, values)
    for copy in key_copies + value_copies:
        copy.start()
    for copy in key_copies:
        copy.wait()
    lane = lax.broadcasted_iota(jnp.int32, (1, width), 1)
    wide = lax.broadcasted_iota(jnp.int32, (BLOCK, width), 1)
    causal = (wide >= BLOCK) | (wide <= lax.broadcasted_iota(jnp.int32, (BLOCK, width), 0))
    groups = tiles // TILES
    steps = heads * groups
    every = range(TILES)

    def fold(op, x):
        return functools.reduce(op, [x[:, a : a + 128] for a in range(0, width, 128)])

    def list_of(step, t):
        return (first_head + step // groups) * tiles + (step % groups) * TILES + t

    def place_of(step, t):
        head = step // groups
        return (
            pl.ds(((step % groups) * TILES + t) * BLOCK, BLOCK),
            pl.ds(pl.multiple_of(head * HEAD_SIZE, HEAD_SIZE), HEAD_SIZE),
        )

    def chunks_of(step):
        counts = [count_ref[list_of(step, t), 0] for t in every]
        return (functools.reduce(jnp.maximum, counts) + CHUNK - 1) // CHUNK

    def gathered(ref, at, c):
        starts = [pl.multiple_of(idx_ref[at, c * CHUNK + j], BLOCK) for j in range(CHUNK)]
        return jnp.concatenate([ref[pl.ds(s, BLOCK), :] for s in starts], axis=0)

    def score(step, side, c, t, best):
        at = list_of(step, t)
        s = lax.dot_general(
            query_ref[place_of(step, t)],
            gathered(keys, at, c),
            (((1,), (1,)), ((), ())),
            preferred_element_type=jnp.float32,
        )
        ok = lane < (count_ref[at, 0] - c * CHUNK) * BLOCK
        if best is None:
            ok = ok & causal
        s = jnp.where(ok, s, NEG_FILL)
        score_s[side][t, c] = s
        top = fold(jnp.maximum, s)
        return top if best is None else jnp.maximum(best, top)

    def mix(step, side, c, t, state):
        shift = jnp.concatenate([shift_s[side][t]] * (width // 128), axis=1)
        p = jnp.exp2(score_s[side][t, c] * SCALE - shift)
        total = fold(jnp.add, p)
        mixed = jnp.dot(
            p.astype(jnp.bfloat16),
            gathered(values, list_of(step, t), c),
            preferred_element_type=jnp.float32,
        )
        return (total, mixed) if state is None else (state[0] + total, state[1] + mixed)

    def settle(side, best):
        for t in every:
            top = jnp.max(best[t], axis=1, keepdims=True) * SCALE
            shift_s[side][t] = jnp.broadcast_to(top, (BLOCK, 128))

    def more_scores(step, side, start, end, best):
        def more(c, best):
            return tuple(score(step, side, c, t, best[t]) for t in every)

        return lax.fori_loop(start, end, more, best)

    best = tuple(score(0, 0, 0, t, None) for t in every)
    settle(0, more_scores(0, 0, 1, chunks_of(0), best))
    for copy in value_copies:
        copy.wait()

    def one_step(step, side):
        other = 1 - side
        later = jnp.minimum(step + 1, steps - 1)
        here = chunks_of(step)
        there = jnp.where(step + 1 < steps, chunks_of(later), 1)
        both = [(mix(step, side, 0, t, None), score(later, other, 0, t, None)) for t in every]

        def fused(c, carried):
            state, best = carried
            both = [
                (mix(step, side, c, t, state[t]), score(later, other, c, t, best[t]))
                for t in every
            ]
            return tuple(x[0] for x in both), tuple(x[1] for x in both)

        shared = jnp.minimum(here, there)
        state, best = lax.fori_loop(
            1, shared, fused, (tuple(x[0] for x in both), tuple(x[1] for x in both))
        )
        state = lax.fori_loop(
            shared, here, lambda c, st: tuple(mix(step, side, c, t, st[t]) for t in every), state
        )
        best = more_scores(later, other, shared, there, best)
        for t in every:
            total, mixed = state[t]
            share = 1.0 / jnp.sum(total, axis=1, keepdims=True)
            out_ref[place_of(step, t)] = (mixed * share).astype(jnp.bfloat16)
        settle(other, best)

    def two_steps(pair, _):
        one_step(2 * pair, 0)
        one_step(2 * pair + 1, 1)
        return 0

    lax.fori_loop(0, steps // 2, two_steps, 0)


def attend(first_head, idx, count, query_rows, key_pieces, value_pieces, key_at, value_at, tokens):
    tiles = query_rows.shape[0] // BLOCK
    heads = query_rows.shape[1] // HEAD_SIZE
    smem = pl.BlockSpec(memory_space=pltpu.SMEM)
    vmem = pl.BlockSpec(memory_space=pltpu.VMEM)
    hbm = pl.BlockSpec(memory_space=pl.ANY)
    return pl.pallas_call(
        functools.partial(attend_kernel, tiles, first_head, heads, key_at, value_at),
        out_shape=jax.ShapeDtypeStruct(query_rows.shape, jnp.bfloat16),
        in_specs=[smem, smem, vmem] + [hbm] * (len(key_pieces) + len(value_pieces)),
        out_specs=vmem,
        scratch_shapes=[
            pltpu.VMEM((tokens, HEAD_SIZE), jnp.bfloat16),
            pltpu.VMEM((tokens, HEAD_SIZE), jnp.bfloat16),
            pltpu.VMEM((TILES, SLOTS // CHUNK, BLOCK, CHUNK * BLOCK), jnp.float32),
            pltpu.VMEM((TILES, SLOTS // CHUNK, BLOCK, CHUNK * BLOCK), jnp.float32),
            pltpu.VMEM((TILES, BLOCK, 128), jnp.float32),
            pltpu.VMEM((TILES, BLOCK, 128), jnp.float32),
            pltpu.SemaphoreType.DMA((sum(len(x) for x in key_at + value_at),)),
        ],
        compiler_params=pltpu.CompilerParams(vmem_limit_bytes=40 << 20),
    )(idx, count, query_rows, *key_pieces, *value_pieces)


def shifted(x, axis, size, by):
    return lax.ppermute(x, axis, [(i, (i + by) % size) for i in range(size)])


def ring_slot(distance, size):
    step = distance % size
    return jnp.where(step == 3, 1, jnp.where(step == 0, 0, step + 1))


def both_ways(xs, axes, beside=()):
    out = [shifted(x, axis, 4, by) for x, axis in zip(xs, axes) for by in (1, -1)]
    out = lax.optimization_barrier(tuple(xs) + tuple(out) + tuple(beside))
    xs, out, beside = out[:2], out[2:6], out[6:]
    return xs, out[::2], out[1::2], beside


def onward(previous, following, axes):
    out = []
    for p, f, axis in zip(previous, following, axes):
        half = p.shape[0] // 2
        out.append(shifted(p[:half], axis, 4, 1))
        out.append(shifted(f[half:], axis, 4, -1))
    return out


def list_kernel(sizes, vertical_s, vertical_ref, slash_ref, idx_ref, count_ref):
    planes, across, cores, reps = sizes
    z, x = lax.axis_index("z"), lax.axis_index("x")
    core, y = lax.axis_index("core"), lax.axis_index("rep")
    per = ROWS // BLOCK
    tiles = planes * per
    slots = SLOTS // 2
    tile = lax.broadcasted_iota(jnp.int32, (tiles, slots), 0)
    strip = ((y * planes + tile // per) * across + x) * cores + core
    blocks = strip * per + tile % per
    earlier = lax.broadcasted_iota(jnp.int32, (slots, slots), 0) < lax.broadcasted_iota(
        jnp.int32, (slots, slots), 1
    )
    earlier = earlier.astype(jnp.float32)
    slot = lax.broadcasted_iota(jnp.int32, (tiles, SLOTS), 1)
    first = pl.multiple_of(z * HEADS, HEADS)
    vertical = vertical_ref[pl.ds(first, HEADS), :]
    slash = slash_ref[pl.ds(first, HEADS), :]

    def place_of(picks):
        picks = jnp.maximum(picks, 0)
        strip = picks // per
        core_of = (strip + core) % cores
        x_of = ring_slot(strip // cores - x + across, across)
        z_of = strip // (cores * across) % planes
        y_of = ring_slot(strip // (cores * across * planes) - y + reps, reps)
        at = ((core_of * reps + y_of) * across + x_of) * planes + z_of
        return (at * per + picks % per) * BLOCK

    for head in range(HEADS):
        columns = jnp.broadcast_to(vertical[head : head + 1], (tiles, slots))
        offsets = jnp.broadcast_to(slash[head : head + 1], (tiles, slots))
        sources = blocks - offsets
        repeated = jnp.zeros((tiles, slots), jnp.int32)
        for j in range(slots):
            same = sources == vertical_s[z * HEADS + head, j]
            repeated = jnp.where(same, 1, repeated)
        keep = (offsets >= 0) & (sources >= 0) & ((offsets == 0) | (repeated == 0))
        total = jnp.zeros((tiles, 1), jnp.int32)
        idx = jnp.zeros((tiles, SLOTS), jnp.int32)
        for picks, ok in ((sources, keep), (columns, (columns >= 0) & (columns < blocks))):
            taken = jnp.where(ok, 1.0, 0.0)
            before = jnp.dot(taken, earlier, preferred_element_type=jnp.float32)
            goes = jnp.where(ok, before.astype(jnp.int32) + total, -1)
            at = place_of(picks)
            for j in range(slots):
                hit = goes[:, j : j + 1] == slot
                idx = jnp.where(hit, at[:, j : j + 1], idx)
            total = total + jnp.sum(taken, axis=1, keepdims=True).astype(jnp.int32)
        rows = pl.ds(head * tiles, tiles)
        idx_ref[rows, :] = idx
        count_ref[rows, :] = jnp.broadcast_to(total, (tiles, 8))


def block_lists(vertical, slash, sizes):
    tiles = sizes[0] * ROWS // BLOCK
    vmem = pl.BlockSpec(memory_space=pltpu.VMEM)
    return pl.pallas_call(
        functools.partial(list_kernel, sizes),
        out_shape=(
            jax.ShapeDtypeStruct((HEADS * tiles, SLOTS), jnp.int32),
            jax.ShapeDtypeStruct((HEADS * tiles, 8), jnp.int32),
        ),
        in_specs=[pl.BlockSpec(memory_space=pltpu.SMEM), vmem, vmem],
        out_specs=(vmem, vmem),
    )(vertical, vertical, slash)


def body(sizes, queries, keys, values, vertical, slash):
    planes, across, cores, reps = sizes
    idx, count = block_lists(vertical, slash, sizes)

    def regroup(x):
        return lax.all_to_all(x, "z", split_axis=0, concat_axis=0, tiled=True)

    def by_plane(x):
        return x.reshape(ROWS, planes, -1).transpose(1, 0, 2)

    pair = regroup(jnp.concatenate([by_plane(keys), by_plane(values)], axis=1))
    own = planes * ROWS
    key_rows = pair[:, :ROWS].reshape(own, HEAD_SIZE)
    value_rows = pair[:, ROWS:].reshape(own, HEAD_SIZE)
    axes = ("x", "rep")
    xs, previous, following, _ = both_ways((key_rows, value_rows), axes)
    far = lax.optimization_barrier(tuple(onward(previous, following, axes)))
    xs = [
        jnp.concatenate([xs[i], previous[i], following[i], far[2 * i], far[2 * i + 1]], axis=0)
        for i in range(2)
    ]
    axes = ("rep", "x")
    *xs, queries = lax.optimization_barrier((*xs, queries))
    query_rows = regroup(by_plane(queries)).reshape(own, HEADS * HEAD_SIZE)
    cuts = [a * HEAD_SIZE for a in HEAD_CUTS]
    query_parts = [query_rows[:, a:b] for a, b in zip(cuts, cuts[1:])]
    beside = (idx, count, *[shifted(x, "core", cores, 1) for x in xs])
    xs, previous, following, beside = both_ways(xs, axes, beside)
    idx, count, *across_core = beside
    far = onward(previous, following, axes)
    pieces = []
    for i in range(2):
        near = [xs[i], previous[i], following[i]]
        other = [across_core[i]] + [shifted(p, "core", cores, 1) for p in near[1:]]
        pieces.append((near + far[2 * i : 2 * i + 2], other))
    far = lax.optimization_barrier(tuple(far))
    for i in range(2):
        last = [shifted(p, "core", cores, 1) for p in far[2 * i : 2 * i + 2]]
        pieces[i] = pieces[i][0] + pieces[i][1] + last
    key_pieces, value_pieces = pieces

    key_at, value_at = [], []
    place = 0
    for piece in key_pieces:
        key_at.append([(0, place, piece.shape[0])])
        place += piece.shape[0]
    place = 0
    for piece in value_pieces:
        parts = []
        for a in range(0, piece.shape[0], own):
            core_of, rest = divmod((place + a) // own, across * reps)
            x_of, y_of = divmod(rest, reps)
            parts.append((a, ((core_of * reps + y_of) * across + x_of) * own, own))
        value_at.append(parts)
        place += piece.shape[0]

    outs = []
    first_head = 0
    for query_rows in query_parts:
        out = attend(
            first_head, idx, count, query_rows, key_pieces, value_pieces, key_at, value_at, place
        )
        first_head += query_rows.shape[1] // HEAD_SIZE
        outs.append(regroup(out.reshape(planes, ROWS, query_rows.shape[1])))
    out = jnp.concatenate(outs, axis=2)
    return out.transpose(1, 0, 2).reshape(ROWS, QUERY_HEADS * HEAD_SIZE)


def solution(mesh):
    reps = mesh.devices.shape[1]
    sizes = (8, 4, 2, reps)
    split = Mesh(mesh.devices.reshape(sizes), ("z", "x", "core", "rep"))
    rows = P(("rep", "z", "x", "core"), None)
    return jax.shard_map(
        functools.partial(body, sizes),
        mesh=split,
        in_specs=(rows, rows, rows, P(), P()),
        out_specs=rows,
        check_vma=False,
    )
```

```python
import functools
import math

import jax
import jax.numpy as jnp
from jax import lax
from jax.experimental import pallas as pl
from jax.experimental.pallas import tpu as pltpu
from jax.sharding import Mesh, PartitionSpec as P

QUERY_HEADS = 64
KEY_VALUE_HEADS = 8
HEADS = QUERY_HEADS // KEY_VALUE_HEADS
HEAD_SIZE = 128
BLOCK = 64
ROWS = 128
SLOTS = 48
TILES = 8
CHUNK = 8
HEAD_CUTS = (0, 5, 8)
NEG_FILL = -1e30
SCALE = math.log2(math.e) / math.sqrt(HEAD_SIZE)


def attend_kernel(
    tiles, first_head, heads, key_at, value_at, idx_ref, count_ref, query_ref, *refs
):
    pieces, refs = refs[: len(key_at) + len(value_at)], refs[len(key_at) + len(value_at) :]
    out_ref, keys, values, scores_a, scores_b, shift_a, shift_b, sem = refs
    score_s, shift_s = (scores_a, scores_b), (shift_a, shift_b)
    width = CHUNK * BLOCK
    slots = iter(range(sem.shape[0]))

    def copies(sources, places, target):
        return [
            pltpu.make_async_copy(
                source.at[pl.ds(a, n), :], target.at[pl.ds(b, n), :], sem.at[next(slots)]
            )
            for source, place in zip(sources, places)
            for a, b, n in place
        ]

    key_copies = copies(pieces[: len(key_at)], key_at, keys)
    value_copies = copies(pieces[len(key_at) :], value_at, values)
    for copy in key_copies + value_copies:
        copy.start()
    for copy in key_copies:
        copy.wait()
    lane = lax.broadcasted_iota(jnp.int32, (1, width), 1)
    wide = lax.broadcasted_iota(jnp.int32, (BLOCK, width), 1)
    causal = (wide >= BLOCK) | (wide <= lax.broadcasted_iota(jnp.int32, (BLOCK, width), 0))
    groups = tiles // TILES
    steps = heads * groups
    every = range(TILES)

    def fold(op, x):
        return functools.reduce(op, [x[:, a : a + 128] for a in range(0, width, 128)])

    def list_of(step, t):
        return (first_head + step // groups) * tiles + (step % groups) * TILES + t

    def place_of(step, t):
        head = step // groups
        return (
            pl.ds(((step % groups) * TILES + t) * BLOCK, BLOCK),
            pl.ds(pl.multiple_of(head * HEAD_SIZE, HEAD_SIZE), HEAD_SIZE),
        )

    def chunks_of(step):
        counts = [count_ref[list_of(step, t), 0] for t in every]
        return (functools.reduce(jnp.maximum, counts) + CHUNK - 1) // CHUNK

    def gathered(ref, at, c):
        starts = [pl.multiple_of(idx_ref[at, c * CHUNK + j], BLOCK) for j in range(CHUNK)]
        return jnp.concatenate([ref[pl.ds(s, BLOCK), :] for s in starts], axis=0)

    def score(step, side, c, t, best):
        at = list_of(step, t)
        s = lax.dot_general(
            query_ref[place_of(step, t)],
            gathered(keys, at, c),
            (((1,), (1,)), ((), ())),
            preferred_element_type=jnp.float32,
        )
        ok = lane < (count_ref[at, 0] - c * CHUNK) * BLOCK
        if best is None:
            ok = ok & causal
        s = jnp.where(ok, s, NEG_FILL)
        score_s[side][t, c] = s
        top = fold(jnp.maximum, s)
        return top if best is None else jnp.maximum(best, top)

    def mix(step, side, c, t, state):
        shift = jnp.concatenate([shift_s[side][t]] * (width // 128), axis=1)
        p = jnp.exp2(score_s[side][t, c] * SCALE - shift)
        total = fold(jnp.add, p)
        mixed = jnp.dot(
            p.astype(jnp.bfloat16),
            gathered(values, list_of(step, t), c),
            preferred_element_type=jnp.float32,
        )
        return (total, mixed) if state is None else (state[0] + total, state[1] + mixed)

    def settle(side, best):
        for t in every:
            top = jnp.max(best[t], axis=1, keepdims=True) * SCALE
            shift_s[side][t] = jnp.broadcast_to(top, (BLOCK, 128))

    def more_scores(step, side, start, end, best):
        def more(c, best):
            return tuple(score(step, side, c, t, best[t]) for t in every)

        return lax.fori_loop(start, end, more, best)

    best = tuple(score(0, 0, 0, t, None) for t in every)
    settle(0, more_scores(0, 0, 1, chunks_of(0), best))
    for copy in value_copies:
        copy.wait()

    def one_step(step, side):
        other = 1 - side
        later = jnp.minimum(step + 1, steps - 1)
        here = chunks_of(step)
        there = jnp.where(step + 1 < steps, chunks_of(later), 1)
        both = [(mix(step, side, 0, t, None), score(later, other, 0, t, None)) for t in every]

        def fused(c, carried):
            state, best = carried
            both = [
                (mix(step, side, c, t, state[t]), score(later, other, c, t, best[t]))
                for t in every
            ]
            return tuple(x[0] for x in both), tuple(x[1] for x in both)

        shared = jnp.minimum(here, there)
        state, best = lax.fori_loop(
            1, shared, fused, (tuple(x[0] for x in both), tuple(x[1] for x in both))
        )
        state = lax.fori_loop(
            shared, here, lambda c, st: tuple(mix(step, side, c, t, st[t]) for t in every), state
        )
        best = more_scores(later, other, shared, there, best)
        for t in every:
            total, mixed = state[t]
            share = 1.0 / jnp.sum(total, axis=1, keepdims=True)
            out_ref[place_of(step, t)] = (mixed * share).astype(jnp.bfloat16)
        settle(other, best)

    def two_steps(pair, _):
        one_step(2 * pair, 0)
        one_step(2 * pair + 1, 1)
        return 0

    lax.fori_loop(0, steps // 2, two_steps, 0)


def attend(first_head, idx, count, query_rows, key_pieces, value_pieces, key_at, value_at, tokens):
    tiles = query_rows.shape[0] // BLOCK
    heads = query_rows.shape[1] // HEAD_SIZE
    smem = pl.BlockSpec(memory_space=pltpu.SMEM)
    vmem = pl.BlockSpec(memory_space=pltpu.VMEM)
    hbm = pl.BlockSpec(memory_space=pl.ANY)
    return pl.pallas_call(
        functools.partial(attend_kernel, tiles, first_head, heads, key_at, value_at),
        out_shape=jax.ShapeDtypeStruct(query_rows.shape, jnp.bfloat16),
        in_specs=[smem, smem, vmem] + [hbm] * (len(key_pieces) + len(value_pieces)),
        out_specs=vmem,
        scratch_shapes=[
            pltpu.VMEM((tokens, HEAD_SIZE), jnp.bfloat16),
            pltpu.VMEM((tokens, HEAD_SIZE), jnp.bfloat16),
            pltpu.VMEM((TILES, SLOTS // CHUNK, BLOCK, CHUNK * BLOCK), jnp.float32),
            pltpu.VMEM((TILES, SLOTS // CHUNK, BLOCK, CHUNK * BLOCK), jnp.float32),
            pltpu.VMEM((TILES, BLOCK, 128), jnp.float32),
            pltpu.VMEM((TILES, BLOCK, 128), jnp.float32),
            pltpu.SemaphoreType.DMA((sum(len(x) for x in key_at + value_at),)),
        ],
        compiler_params=pltpu.CompilerParams(vmem_limit_bytes=40 << 20),
    )(idx, count, query_rows, *key_pieces, *value_pieces)


def shifted(x, axis, size, by):
    return lax.ppermute(x, axis, [(i, (i + by) % size) for i in range(size)])


def ring_slot(distance, size):
    step = distance % size
    return jnp.where(step == 3, 1, jnp.where(step == 0, 0, step + 1))


def both_ways(xs, axes, beside=()):
    out = [shifted(x, axis, 4, by) for x, axis in zip(xs, axes) for by in (1, -1)]
    out = lax.optimization_barrier(tuple(xs) + tuple(out) + tuple(beside))
    xs, out, beside = out[:2], out[2:6], out[6:]
    return xs, out[::2], out[1::2], beside


def onward(previous, following, axes):
    out = []
    for p, f, axis in zip(previous, following, axes):
        half = p.shape[0] // 2
        out.append(shifted(p[:half], axis, 4, 1))
        out.append(shifted(f[half:], axis, 4, -1))
    return out


def list_kernel(sizes, vertical_s, vertical_ref, slash_ref, idx_ref, count_ref):
    planes, across, cores, reps = sizes
    z, x = lax.axis_index("z"), lax.axis_index("x")
    core, y = lax.axis_index("core"), lax.axis_index("rep")
    per = ROWS // BLOCK
    tiles = planes * per
    slots = SLOTS // 2
    tile = lax.broadcasted_iota(jnp.int32, (tiles, slots), 0)
    strip = ((y * planes + tile // per) * across + x) * cores + core
    blocks = strip * per + tile % per
    earlier = lax.broadcasted_iota(jnp.int32, (slots, slots), 0) < lax.broadcasted_iota(
        jnp.int32, (slots, slots), 1
    )
    earlier = earlier.astype(jnp.float32)
    slot = lax.broadcasted_iota(jnp.int32, (tiles, SLOTS), 1)
    first = pl.multiple_of(z * HEADS, HEADS)
    vertical = vertical_ref[pl.ds(first, HEADS), :]
    slash = slash_ref[pl.ds(first, HEADS), :]

    def place_of(picks):
        picks = jnp.maximum(picks, 0)
        strip = picks // per
        core_of = (strip + core) % cores
        x_of = ring_slot(strip // cores - x + across, across)
        z_of = strip // (cores * across) % planes
        y_of = ring_slot(strip // (cores * across * planes) - y + reps, reps)
        at = ((core_of * reps + y_of) * across + x_of) * planes + z_of
        return (at * per + picks % per) * BLOCK

    for head in range(HEADS):
        columns = jnp.broadcast_to(vertical[head : head + 1], (tiles, slots))
        offsets = jnp.broadcast_to(slash[head : head + 1], (tiles, slots))
        sources = blocks - offsets
        repeated = jnp.zeros((tiles, slots), jnp.int32)
        for j in range(slots):
            same = sources == vertical_s[z * HEADS + head, j]
            repeated = jnp.where(same, 1, repeated)
        keep = (offsets >= 0) & (sources >= 0) & ((offsets == 0) | (repeated == 0))
        total = jnp.zeros((tiles, 1), jnp.int32)
        idx = jnp.zeros((tiles, SLOTS), jnp.int32)
        for picks, ok in ((sources, keep), (columns, (columns >= 0) & (columns < blocks))):
            taken = jnp.where(ok, 1.0, 0.0)
            before = jnp.dot(taken, earlier, preferred_element_type=jnp.float32)
            goes = jnp.where(ok, before.astype(jnp.int32) + total, -1)
            at = place_of(picks)
            for j in range(slots):
                hit = goes[:, j : j + 1] == slot
                idx = jnp.where(hit, at[:, j : j + 1], idx)
            total = total + jnp.sum(taken, axis=1, keepdims=True).astype(jnp.int32)
        rows = pl.ds(head * tiles, tiles)
        idx_ref[rows, :] = idx
        count_ref[rows, :] = jnp.broadcast_to(total, (tiles, 8))


def block_lists(vertical, slash, sizes):
    tiles = sizes[0] * ROWS // BLOCK
    vmem = pl.BlockSpec(memory_space=pltpu.VMEM)
    return pl.pallas_call(
        functools.partial(list_kernel, sizes),
        out_shape=(
            jax.ShapeDtypeStruct((HEADS * tiles, SLOTS), jnp.int32),
            jax.ShapeDtypeStruct((HEADS * tiles, 8), jnp.int32),
        ),
        in_specs=[pl.BlockSpec(memory_space=pltpu.SMEM), vmem, vmem],
        out_specs=(vmem, vmem),
    )(vertical, vertical, slash)


def body(sizes, queries, keys, values, vertical, slash):
    planes, across, cores, reps = sizes
    idx, count = block_lists(vertical, slash, sizes)

    def regroup(x):
        return lax.all_to_all(x, "z", split_axis=0, concat_axis=0, tiled=True)

    def by_plane(x):
        return x.reshape(ROWS, planes, -1).transpose(1, 0, 2)

    pair = regroup(jnp.concatenate([by_plane(keys), by_plane(values)], axis=1))
    own = planes * ROWS
    key_rows = pair[:, :ROWS].reshape(own, HEAD_SIZE)
    value_rows = pair[:, ROWS:].reshape(own, HEAD_SIZE)
    axes = ("x", "rep")
    xs, previous, following, _ = both_ways((key_rows, value_rows), axes)
    far = lax.optimization_barrier(tuple(onward(previous, following, axes)))
    xs = [
        jnp.concatenate([xs[i], previous[i], following[i], far[2 * i], far[2 * i + 1]], axis=0)
        for i in range(2)
    ]
    axes = ("rep", "x")
    *xs, queries = lax.optimization_barrier((*xs, queries))
    query_rows = regroup(by_plane(queries)).reshape(own, HEADS * HEAD_SIZE)
    cuts = [a * HEAD_SIZE for a in HEAD_CUTS]
    query_parts = [query_rows[:, a:b] for a, b in zip(cuts, cuts[1:])]
    beside = (idx, count, *[shifted(x, "core", cores, 1) for x in xs])
    xs, previous, following, beside = both_ways(xs, axes, beside)
    idx, count, *across_core = beside
    far = onward(previous, following, axes)
    pieces = []
    for i in range(2):
        near = [xs[i], previous[i], following[i]]
        other = [across_core[i]] + [shifted(p, "core", cores, 1) for p in near[1:]]
        pieces.append((near + far[2 * i : 2 * i + 2], other))
    far = lax.optimization_barrier(tuple(far))
    for i in range(2):
        last = [shifted(p, "core", cores, 1) for p in far[2 * i : 2 * i + 2]]
        pieces[i] = pieces[i][0] + pieces[i][1] + last
    key_pieces, value_pieces = pieces

    key_at, value_at = [], []
    place = 0
    for piece in key_pieces:
        key_at.append([(0, place, piece.shape[0])])
        place += piece.shape[0]
    place = 0
    for piece in value_pieces:
        parts = []
        for a in range(0, piece.shape[0], own):
            core_of, rest = divmod((place + a) // own, across * reps)
            x_of, y_of = divmod(rest, reps)
            parts.append((a, ((core_of * reps + y_of) * across + x_of) * own, own))
        value_at.append(parts)
        place += piece.shape[0]

    outs = []
    first_head = 0
    for query_rows in query_parts:
        out = attend(
            first_head, idx, count, query_rows, key_pieces, value_pieces, key_at, value_at, place
        )
        first_head += query_rows.shape[1] // HEAD_SIZE
        outs.append(regroup(out.reshape(planes, ROWS, query_rows.shape[1])))
    out = jnp.concatenate(outs, axis=2)
    return out.transpose(1, 0, 2).reshape(ROWS, QUERY_HEADS * HEAD_SIZE)


def solution(mesh):
    reps = mesh.devices.shape[1]
    sizes = (8, 4, 2, reps)
    split = Mesh(mesh.devices.reshape(sizes), ("z", "x", "core", "rep"))
    rows = P(("rep", "z", "x", "core"), None)
    return jax.shard_map(
        functools.partial(body, sizes),
        mesh=split,
        in_specs=(rows, rows, rows, P(), P()),
        out_specs=rows,
        check_vma=False,
    )
```
